256 devices in a mesh: grp: 4 (over z_hi), tile: 64 (over x, z_lo, y, core).
Axes of the slice: x: 4, y: 4, z: 8 (z_hi: 4, z_lo: 2; z = z_hi * 2 + z_lo), core: 2. Of those that a mesh axis runs over, the one named last changes fastest.
Arguments:
- ocean_state: bfloat16 [64, 4096, 512], P(None, 'tile', 'grp'), may hold values from -8 to 8
- sea_mask: int32 [4096, 512], P('tile', 'grp'), may hold values 0 or 1
- spectral_weights: float32 [2, 2, 32, 64, 64], replicated, may hold values from -0.75 to 0.75
- point_weights: bfloat16 [2, 64, 64], replicated, may hold values from -0.75 to 0.75
- point_bias: float32 [2, 64], replicated, may hold values from -4 to 4
- inner_weights: bfloat16 [2, 128, 64], replicated, may hold values from -0.75 to 0.75
- outer_weights: bfloat16 [2, 64, 128], replicated, may hold values from -0.5 to 0.5
- coarse_spectral: float32 [2, 32, 64, 64], replicated, may hold values from -0.75 to 0.75
- coarse_point: float32 [64, 64], replicated, may hold values from -0.75 to 0.75
- coarse_bias: float32 [64], replicated, may hold values from -2.5 to 2.5
Outputs:
- corrected: bfloat16 [64, 4096, 512], P(None, 'tile', 'grp')
The draws below stay inside these ranges and needn't reach their ends.
Inputs may be any that keep to these rules, and one draw needn't show every extreme that they name: `sea_mask`: 1 marks a sea cell, 0 a land cell.
All inputs are finite; a program needn't handle non-finite values. No bound on the sum of `sea_mask` on one device may be relied on, other than what follows from the above.
Results may differ from the reference program's by a relative error of at most 0.0065.
Values may be sent and summed in bfloat16 or wider, within the bound.
A program may use at most 64 MiB of HBM per device.

```python
import math
import jax
import jax.numpy as jnp
from jax import lax

C = 64
F = 128
TX = 64
TY = 128
H = 64
R = 16
MX = 8
MY = 4
LAYERS = 2
MODES = 32
NX = 4096
NY = 512
NXC = 256
NYC = 32
N_GRP = 4
N_TILE = 64


def draw_ocean_state(key, part):
    subkeys = jax.random.split(key, 8)
    wave_count = 8
    row_frac = jnp.arange(NX, dtype=jnp.float32)[:, None] / NX
    col_frac = jnp.arange(NY, dtype=jnp.float32)[None, :] / NY
    reach_rows = max(1.0, NX / 48.0)
    reach_cols = max(1.0, NY / 48.0)
    freq_rows = jax.random.uniform(subkeys[0], (wave_count,), minval=0.5, maxval=reach_rows)
    freq_cols = jax.random.uniform(subkeys[1], (wave_count,), minval=-reach_cols, maxval=reach_cols)
    shifts = jax.random.uniform(subkeys[2], (wave_count,))
    amplitude = jax.random.normal(subkeys[3], (C, wave_count)) * 0.6
    smooth = jnp.zeros((C, NX, NY), jnp.float32)
    for wave_index in range(wave_count):
        cycles = freq_rows[wave_index] * row_frac + freq_cols[wave_index] * col_frac + shifts[wave_index]
        cycles = cycles - jnp.floor(cycles)
        smooth = smooth + amplitude[:, wave_index][:, None, None] * jnp.cos(2.0 * math.pi * cycles)[None]
    roughness = jax.random.uniform(subkeys[4], (C, NX, NY), minval=0.5, maxval=1.5)
    block_terms = jax.random.normal(subkeys[7], (C, NX // R, NY // R))
    blocky = jnp.repeat(jnp.repeat(block_terms, R, axis=1), R, axis=2)
    jitter_noise = jax.random.normal(subkeys[6], (C, NX, NY)) * 0.4
    values = smooth * roughness + jitter_noise + blocky
    return jnp.clip(values, -8.0, 8.0).astype(jnp.bfloat16)


def place_ends(array, rng, smallest, high):
    spot = [jax.random.randint(jax.random.fold_in(rng, axis), (), 0, length) for axis, length in enumerate(array.shape)]
    widest = array.shape.index(max(array.shape))
    beside = spot[:widest] + [(spot[widest] + 1) % array.shape[widest]] + spot[widest + 1:]
    return array.at[tuple(spot)].set(smallest).at[tuple(beside)].set(high)


def scatter_about(own_key, shape, spread, limit, kind=jnp.bfloat16):
    return jnp.clip(spread * jax.random.normal(own_key, shape, jnp.float32), -limit, limit).astype(kind)


def setup_inputs(seed: int = 0) -> dict:
    seeds = jax.random.split(jax.random.key(seed), 11)
    ocean_state = draw_ocean_state(jax.random.fold_in(seeds[10], 71), 0)
    sea_mask = place_ends((jax.random.randint(seeds[1], (NX, NY), 0, 4) < 3).astype(jnp.int32), jax.random.fold_in(seeds[1], 1), 0, 1)
    spectral_weights = scatter_about(seeds[2], (LAYERS, 2, MODES, C, C), C ** -0.5, 0.75, jnp.float32)
    point_weights = scatter_about(seeds[3], (LAYERS, C, C), C ** -0.5, 0.75)
    point_bias = scatter_about(seeds[4], (LAYERS, C), 1.0, 4.0, jnp.float32)
    inner_weights = scatter_about(seeds[5], (LAYERS, F, C), C ** -0.5, 0.75)
    outer_weights = scatter_about(seeds[6], (LAYERS, C, F), F ** -0.5, 0.5)
    coarse_spectral = scatter_about(seeds[7], (2, MODES, C, C), C ** -0.5, 0.75, jnp.float32)
    coarse_point = scatter_about(seeds[8], (C, C), C ** -0.5, 0.75, jnp.float32)
    coarse_bias = scatter_about(seeds[9], (C,), 0.5, 2.5, jnp.float32)
    return dict(ocean_state=ocean_state, sea_mask=sea_mask, spectral_weights=spectral_weights, point_weights=point_weights, point_bias=point_bias, inner_weights=inner_weights, outer_weights=outer_weights, coarse_spectral=coarse_spectral, coarse_point=coarse_point, coarse_bias=coarse_bias)


PRECISE = lax.Precision.HIGHEST


def wave_numbers():
    order = jnp.arange(MX, dtype=jnp.int32)
    return jnp.where(order < MX // 2, order, order - MX)


def masked_table(positions, numbers, length):
    cycles = (positions[:, None] * numbers[None, :]) % length
    radians = cycles.astype(jnp.float32) * (2.0 * math.pi / length)
    inside = ((positions >= 0) & (positions < length)).astype(jnp.float32)[:, None]
    return jnp.cos(radians) * inside, jnp.sin(radians) * inside


def columns_transform(values, col_positions, col_length):
    channels, row_count, col_count = values.shape
    cos_cols, sin_cols = masked_table(col_positions, jnp.arange(MY, dtype=jnp.int32), col_length)
    lookup = jnp.concatenate([cos_cols, -sin_cols], axis=1)
    flattened = values.reshape(channels * row_count, col_count)
    return jnp.dot(flattened, lookup, precision=PRECISE).reshape(channels, row_count, 2 * MY)


def rows_transform(y_modes, row_positions, row_length):
    cos_rows, sin_rows = masked_table(row_positions, wave_numbers(), row_length)
    real_in = y_modes[:, :, :MY]
    imag_in = y_modes[:, :, MY:]
    coef_real = jnp.einsum("cxj,xi->cij", real_in, cos_rows, precision=PRECISE) + jnp.einsum("cxj,xi->cij", imag_in, sin_rows, precision=PRECISE)
    coef_imag = jnp.einsum("cxj,xi->cij", imag_in, cos_rows, precision=PRECISE) - jnp.einsum("cxj,xi->cij", real_in, sin_rows, precision=PRECISE)
    return jnp.stack([coef_real, coef_imag])


def forward(values, row_positions, col_positions, row_length, col_length):
    return rows_transform(columns_transform(values, col_positions, col_length), row_positions, row_length)


def mix_modes(coeffs, weights):
    channels = coeffs.shape[1]
    flattened = coeffs.reshape(2, channels, MX * MY)
    weight_real = weights[0]
    weight_imag = weights[1]
    mixed_real = jnp.einsum("koc,ck->ok", weight_real, flattened[0], precision=PRECISE) - jnp.einsum("koc,ck->ok", weight_imag, flattened[1], precision=PRECISE)
    mixed_imag = jnp.einsum("koc,ck->ok", weight_real, flattened[1], precision=PRECISE) + jnp.einsum("koc,ck->ok", weight_imag, flattened[0], precision=PRECISE)
    return mixed_real, mixed_imag


def synthesis(mixed_real, mixed_imag, row_positions, col_positions, row_length, col_length):
    channels = mixed_real.shape[0]
    grid_real = mixed_real.reshape(channels, MX, MY)
    grid_imag = mixed_imag.reshape(channels, MX, MY)
    cos_rows, sin_rows = masked_table(row_positions, wave_numbers(), row_length)
    part_real = jnp.einsum("cij,xi->cxj", grid_real, cos_rows, precision=PRECISE) - jnp.einsum("cij,xi->cxj", grid_imag, sin_rows, precision=PRECISE)
    part_imag = jnp.einsum("cij,xi->cxj", grid_real, sin_rows, precision=PRECISE) + jnp.einsum("cij,xi->cxj", grid_imag, cos_rows, precision=PRECISE)
    cos_cols, sin_cols = masked_table(col_positions, jnp.arange(MY, dtype=jnp.int32), col_length)
    weight = jnp.where(jnp.arange(MY) == 0, 1.0, 2.0).astype(jnp.float32)
    lookup = jnp.concatenate([(cos_cols * weight[None, :]).T, -(sin_cols * weight[None, :]).T], axis=0)
    stacked = jnp.concatenate([part_real, part_imag], axis=2)
    row_count = stacked.shape[1]
    result = jnp.dot(stacked.reshape(channels * row_count, 2 * MY), lookup, precision=PRECISE)
    return result.reshape(channels, row_count, col_positions.shape[0])


def finish_layer(coeffs, interior, own_mask, ext_rows, ext_cols, spec, w_point, b_point, w_in, w_out):
    channels, tile_rows, tile_cols = interior.shape
    cell_count = tile_rows * tile_cols
    mixed_real, mixed_imag = mix_modes(coeffs, spec)
    spectral = synthesis(mixed_real, mixed_imag, H + jnp.arange(tile_rows, dtype=jnp.int32), H + jnp.arange(tile_cols, dtype=jnp.int32), ext_rows, ext_cols)
    pre_act = spectral.reshape(channels, cell_count) + jnp.dot(w_point, interior.reshape(channels, cell_count), preferred_element_type=jnp.float32) + b_point[:, None]
    activated = jax.nn.gelu(pre_act, approximate=True).astype(jnp.bfloat16)
    hidden = jax.nn.gelu(jnp.dot(w_in, activated, preferred_element_type=jnp.float32), approximate=True).astype(jnp.bfloat16)
    result = jnp.dot(w_out, hidden, preferred_element_type=jnp.float32) * own_mask.reshape(1, cell_count).astype(jnp.float32)
    return result.reshape(channels, tile_rows, tile_cols).astype(jnp.bfloat16)


def fine_layer(current, sea_mask, spec, w_point, b_point, w_in, w_out):
    channels = current.shape[0]
    ext_rows = TX + 2 * H
    ext_cols = TY + 2 * H
    padded = jnp.pad(current, ((0, 0), (H, H), (H, H)))

    def one_tile(tile_number):
        row_first = (tile_number // N_GRP) * TX
        col_first = (tile_number % N_GRP) * TY
        anchor = jnp.zeros((), jnp.int32)
        extended = lax.dynamic_slice(padded, (anchor, row_first, col_first), (channels, ext_rows, ext_cols))
        interior = lax.dynamic_slice(current, (anchor, row_first, col_first), (channels, TX, TY))
        own_mask = lax.dynamic_slice(sea_mask, (row_first, col_first), (TX, TY))
        coeffs = forward(extended.astype(jnp.float32), jnp.arange(ext_rows, dtype=jnp.int32), jnp.arange(ext_cols, dtype=jnp.int32), ext_rows, ext_cols)
        coeffs = coeffs / (ext_rows * ext_cols)
        return finish_layer(coeffs, interior, own_mask, ext_rows, ext_cols, spec, w_point, b_point, w_in, w_out)

    tile_outputs = lax.map(one_tile, jnp.arange(N_TILE * N_GRP, dtype=jnp.int32))
    arranged = tile_outputs.reshape(N_TILE, N_GRP, channels, TX, TY).transpose(2, 0, 3, 1, 4)
    return arranged.reshape(channels, N_TILE * TX, N_GRP * TY)


def reference(ocean_state, sea_mask, spectral_weights, point_weights, point_bias, inner_weights, outer_weights, coarse_spectral, coarse_point, coarse_bias):
    channels = ocean_state.shape[0]
    current = jnp.where(sea_mask[None] > 0, ocean_state, jnp.zeros((), jnp.bfloat16))
    for layer_index in range(LAYERS):
        current = fine_layer(current, sea_mask, spectral_weights[layer_index], point_weights[layer_index], point_bias[layer_index], inner_weights[layer_index], outer_weights[layer_index])
    fine_values = current.astype(jnp.float32)
    coarse = fine_values.reshape(channels, NXC, R, NYC, R).sum(axis=(2, 4)) / (R * R)
    row_positions = jnp.arange(NXC, dtype=jnp.int32)
    col_positions = jnp.arange(NYC, dtype=jnp.int32)
    coeffs = forward(coarse, row_positions, col_positions, NXC, NYC) / (NXC * NYC)
    mixed_real, mixed_imag = mix_modes(coeffs, coarse_spectral)
    spectral = synthesis(mixed_real, mixed_imag, row_positions, col_positions, NXC, NYC)
    local_term = jnp.dot(coarse_point, coarse.reshape(channels, NXC * NYC), precision=PRECISE)
    correction = spectral + local_term.reshape(channels, NXC, NYC) + coarse_bias[:, None, None]
    land_sea = sea_mask.astype(jnp.float32).reshape(1, NXC, R, NYC, R)
    corrected = fine_values.reshape(channels, NXC, R, NYC, R) + correction[:, :, None, :, None] * land_sea
    return corrected.reshape(channels, NX, NY).astype(jnp.bfloat16)
```

```python
import functools
import math

import jax
import jax.numpy as jnp
import numpy as np
from jax import lax
from jax.experimental import pallas as pl
from jax.experimental.pallas import tpu as pltpu
from jax.sharding import PartitionSpec as P

MESH = pl.DeviceIdType.MESH
F32 = jnp.float32
BF16 = jnp.bfloat16
PRECISE = lax.Precision.HIGHEST

C = 64
F = 128
TX = 64
TY = 128
L1 = 192
L2 = 256
NT = 64
NG = 4
PAD = 72
GROUPS = 8
GELU0 = math.sqrt(2.0 / math.pi)
GELU1 = GELU0 * 0.044715


def lane_numbers():
    lane = np.arange(128)
    ri, half, k = lane // 64, (lane // 32) % 2, lane % 32
    i, j = k // 4, k % 4
    kappa = np.where(i < 4, i, i - 8)
    return ri, half, kappa, j


def constants():
    ri, half, kappa, j = lane_numbers()
    two_pi = 2.0 * np.pi
    cell = np.arange(1024)
    b, q = cell // 128, cell % 128

    phi = two_pi * (b[:, None] * kappa / L1 + (q % 64)[:, None] * j / L2)
    table = np.where(ri == 0, np.cos(phi), -np.sin(phi)) * ((q // 64)[:, None] == half)

    rows = np.arange(64)
    ri_r, k_r = rows // 32, rows % 32
    i_r, j_r = k_r // 4, k_r % 4
    kap_r = np.where(i_r < 4, i_r, i_r - 8)
    phi = two_pi * (kap_r[:, None] * (64 + b) / L1 + j_r[:, None] * (64 + q) / L2)
    basis = np.where(ri_r[:, None] == 0, np.cos(phi), -np.sin(phi))

    pool = ((np.arange(128) % 8)[None, :] == (q // 16)[:, None]) & (np.arange(128) < 32)[None, :]

    def forward(theta):
        return np.cos(theta), np.where(ri == 0, 1.0, -1.0) * np.sin(theta)

    weight = np.where(j == 0, 1.0, 2.0)
    rot = []
    for a in range(GROUPS):
        rot += list(forward(two_pi * kappa * a / 24))
    for rho in range(3):
        rot += list(forward(two_pi * kappa * rho / 3))
    rot += list(forward(two_pi * j * np.where(half == 0, 1, 2) / 4))
    rot += list(forward(two_pi * j * np.where(half == 0, 3, 0) / 4))
    for a in range(GROUPS):
        cos, sin = forward(two_pi * kappa * a / 24)
        rot += [cos * weight / (L1 * L2), -sin * weight / (L1 * L2)]
    rot = np.stack(rot)
    rot = np.concatenate([rot, np.zeros((48 - rot.shape[0], 128))])

    small = np.arange(128)
    br, bq = small // 8, small % 8
    theta = two_pi * (br[:, None] * kappa / 256 + bq[:, None] * j / 32)
    ctab = np.where(ri == 0, np.cos(theta), -np.sin(theta)) * (small < 32)[:, None]
    wide = np.arange(512)
    wr, wq = wide // 128, (wide % 128) // 16
    theta = two_pi * (kappa[:, None] * wr / 256 + j[:, None] * wq / 32)
    stab = np.where(ri[:, None] == 0, np.cos(theta), -np.sin(theta)) * weight[:, None] / (256 * 32)
    stab = stab * (half == 0)[:, None]
    spread = ((br[:, None] == wr) & (bq[:, None] == wq) & (small < 32)[:, None])

    place = np.zeros((64, 128))
    for c in range(64):
        place[c, (32 + c) if c < 32 else (64 + c)] = 1.0

    dev = np.zeros((NT * NG, 2, 128))
    for t in range(NT):
        for g in range(NG):
            dev[t * NG + g, 0], dev[t * NG + g, 1] = forward(two_pi * ((kappa * t % 64) / 64 + (j * g % 4) / 4))
    return dict(
        table=table.astype(BF16),
        basis=basis.astype(BF16),
        pool=pool.astype(np.float32).astype(BF16),
        rot=rot.astype(np.float32),
        ctab=ctab.astype(np.float32),
        stab=stab.astype(np.float32),
        spread=spread.astype(np.float32),
        place=place.astype(BF16),
        dev=dev.astype(np.float32),
    )


ROW3, OWN, REC, SYN = 16, 22, 24, 26


def gelu(v):
    half = 0.5 * v
    return half + half * jnp.tanh(v * (GELU0 + GELU1 * (v * v)))


def dot(a, b):
    return jnp.dot(a, b, preferred_element_type=F32)


def exact(a, b):
    return jnp.dot(a, b, precision=PRECISE, preferred_element_type=F32)


def kernel(
    x_ref, mask_ref, w_ref, wp_ref, bp_ref, win_ref, wout_ref, wc_ref, cp_ref, cb_ref,
    table, basis, pool, rot, ctab, stab, spread, place, dev_ref,
    out_ref,
    xs, mf, fa, fb, wv, lhs, wpad, bias, pbuf, vrecv, hsend, hrecv, csend, crecv, local, cx, devv,
    wsem, ssem, rsem,
):
    t = lax.axis_index("tile")
    g = lax.axis_index("grp")

    weights = [pltpu.make_async_copy(w_ref.at[l], wv.at[l], wsem.at[l]) for l in range(2)]
    weights.append(pltpu.make_async_copy(wc_ref, wv.at[2], wsem.at[2]))
    phase = pltpu.make_async_copy(dev_ref.at[t * NG + g], devv, wsem.at[3])
    for copy in weights:
        copy.start()
    phase.start()

    def at(tile, grp):
        return {"tile": tile, "grp": grp}

    up, down = at(lax.rem(t + NT - 1, NT), g), at(lax.rem(t + 1, NT), g)
    left, right = at(t, lax.rem(g + NG - 1, NG)), at(t, lax.rem(g + 1, NG))
    yc, xc = lax.rem(t, 8), lax.div(t, 16)
    zc = 2 * g + lax.rem(lax.div(t, 8), 2)
    flat = [at(t - yc + lax.rem(yc + d, 8), g) for d in range(1, 8)]
    along_x = [at(lax.rem(xc + d, 4) * 16 + lax.rem(t, 16), g) for d in range(1, 4)]
    along_z = []
    for d in range(1, 8):
        z = lax.rem(zc + d, 8)
        along_z.append(at(xc * 16 + lax.rem(z, 2) * 8 + yc, lax.div(z, 2)))

    barrier = pltpu.get_barrier_semaphore()
    partners = [up, down, left, right] + flat + along_x + along_z
    for partner in partners:
        pl.semaphore_signal(barrier, inc=1, device_id=partner, device_id_type=MESH)

    lane = lax.broadcasted_iota(jnp.int32, (64, 128), 1)
    mode = lane % 32
    in_a = (lane // 32) % 2 == 0
    in_a32 = in_a[:32]
    re_sign = jnp.where(lane < 64, -1.0, 1.0).astype(F32)

    def turned(v, row):
        return v * rot[row : row + 1, :] + pltpu.roll(v, 64, 1) * rot[row + 1 : row + 2, :]

    mf[...] = mask_ref[...].astype(F32)

    def mask_step(c, carry):
        xs[pl.ds(pl.multiple_of(c * PAD, 8), 64), :] = jnp.where(mask_ref[...] > 0, x_ref[c].astype(F32), 0.0)
        return carry

    lax.fori_loop(0, C, mask_step, 0, unroll=4)

    def analysis(field, a, total):
        part = dot(field[a], table[...])
        cos = rot[pl.ds(2 * a, 1), :]
        sin = rot[pl.ds(2 * a + 1, 1), :]
        return total + part * cos + pltpu.roll(part, 64, 1) * sin

    def group_step(a, total):
        for b in range(8):
            fa[a, :, b * 128 : (b + 1) * 128] = xs[pl.ds(8 * a + b, 64, stride=PAD), :].astype(BF16)
        return analysis(fa, a, total)

    total = lax.fori_loop(0, GROUPS, group_step, jnp.zeros((64, 128), F32))

    eye = lax.broadcasted_iota(jnp.int32, (64, 64), 0) == lax.broadcasted_iota(jnp.int32, (64, 64), 1)

    def column(row):
        return jnp.broadcast_to(jnp.sum(jnp.where(eye, row, 0.0), axis=1, keepdims=True), (64, 128))

    for l in range(2):
        wpad[l] = dot(wp_ref[l], place[...])
        bias[l] = column(bp_ref[l : l + 1, :])
    bias[2] = column(cb_ref[...])

    def remote(src, dst, number, device):
        return pltpu.make_async_remote_copy(
            src_ref=src, dst_ref=dst, send_sem=ssem.at[number], recv_sem=rsem.at[number],
            device_id=device, device_id_type=MESH,
        )

    def exchange(l, total):
        pbuf[l] = total
        sends = [
            remote(pbuf.at[l], vrecv.at[l, 1], 4 * l, up),
            remote(pbuf.at[l], vrecv.at[l, 0], 4 * l + 1, down),
        ]
        for s in sends:
            s.start()
        own = turned(total, ROW3 + 2)
        for s in sends:
            s.wait()
        above = jnp.where(t > 0, vrecv[l, 0], 0.0)
        below = jnp.where(t < NT - 1, vrecv[l, 1], 0.0)
        v = own + turned(above, ROW3) + turned(below, ROW3 + 4)
        hsend[l, 0] = jnp.where(in_a32, v[:32], pltpu.roll(v[32:], 32, 1))
        hsend[l, 1] = jnp.where(in_a32, pltpu.roll(v[:32], 96, 1), v[32:])
        sends = [
            remote(hsend.at[l, 0], hrecv.at[l, 0], 4 * l + 2, left),
            remote(hsend.at[l, 1], hrecv.at[l, 1], 4 * l + 3, right),
        ]
        for s in sends:
            s.start()
        own = turned(v, OWN)
        for s in sends:
            s.wait()
        from_right = jnp.where(g < NG - 1, hrecv[l, 0], 0.0)
        from_left = jnp.where(g > 0, hrecv[l, 1], 0.0)
        first = jnp.concatenate([from_right, pltpu.roll(from_right, 96, 1)], axis=0)
        second = jnp.concatenate([pltpu.roll(from_left, 32, 1), from_left], axis=0)
        both = own + turned(jnp.where(in_a, first, second), REC)
        return both + pltpu.roll(both, 96, 1)

    def mix(l, u):
        plain = u.astype(BF16)
        crossed = (pltpu.roll(u, 64, 1) * re_sign).astype(BF16)
        acc = jnp.zeros((64, 128), F32)
        for block in range(8):
            rows = slice(block * 256, (block + 1) * 256)
            o = dot(wv[l, 0, rows, :].astype(BF16), plain) + dot(wv[l, 1, rows, :].astype(BF16), crossed)
            for n in range(4):
                acc = acc + jnp.where(mode == block * 4 + n, o[n * 64 : (n + 1) * 64], 0.0)
        return acc

    def layer(l, src, dst, v, per_group, start):
        for a in range(GROUPS):
            lhs[a] = jnp.where(in_a, turned(v, SYN + 2 * a), wpad[l]).astype(BF16)

        def step(a, total):
            for n in range(4):
                cols = slice(n * 256, (n + 1) * 256)
                rhs = jnp.concatenate(
                    [basis[:32, cols], src[a, :32, cols], basis[32:, cols], src[a, 32:, cols]], axis=0
                )
                shift = jnp.concatenate([bias[l], bias[l]], axis=1)
                act = gelu(dot(lhs[a], rhs) + shift).astype(BF16)
                hid = gelu(dot(win_ref[l], act)).astype(BF16)
                sea = jnp.concatenate(
                    [mf[pl.ds(8 * a + 2 * n, 1), :], mf[pl.ds(8 * a + 2 * n + 1, 1), :]], axis=1
                )
                dst[a, :, cols] = (dot(wout_ref[l], hid) * sea).astype(BF16)
            return per_group(dst, a, total)

        return lax.fori_loop(0, GROUPS, step, start)

    pl.semaphore_wait(barrier, len(partners))
    u = exchange(0, total)
    weights[0].wait()
    v = mix(0, u)
    total = layer(0, fa, fb, v, analysis, jnp.zeros((64, 128), F32))
    u = exchange(1, total)
    weights[1].wait()
    v = mix(1, u)

    def pooled(field, a, total):
        return total + jnp.where(lane // 8 == a // 2, dot(field[a], pool[...]), 0.0)

    coarse = layer(1, fb, fa, v, pooled, jnp.zeros((64, 128), F32)) * (1.0 / 256.0)

    phase.wait()
    cos, sin = devv[0:1, :], devv[1:2, :]
    part = exact(coarse, ctab[...])
    part = part * cos + pltpu.roll(part, 64, 1) * sin
    acc = jnp.where(in_a32, part[:32], part[32:])
    number, slot = 8, 0
    for stage, peers in enumerate((flat, along_x, along_z)):
        csend[stage] = acc
        sends = []
        for peer in peers:
            sends.append(remote(csend.at[stage], crecv.at[slot], number, peer))
            number, slot = number + 1, slot + 1
        for s in sends:
            s.start()
        if stage == 0:
            local[...] = exact(cp_ref[...], exact(coarse, spread[...])) + jnp.concatenate([bias[2]] * 4, axis=1)
        if stage == 2:
            def back_step(a, carry):
                for b in range(8):
                    xs[pl.ds(8 * a + b, 64, stride=PAD), :] = fa[a, :, b * 128 : (b + 1) * 128].astype(F32)
                return carry

            lax.fori_loop(0, GROUPS, back_step, 0)
        for s in sends:
            s.wait()
        for n in range(slot - len(peers), slot):
            acc = acc + crecv[n]
    u = jnp.concatenate([acc, pltpu.roll(acc, 96, 1)], axis=0)
    weights[2].wait()
    v = mix(2, u)
    v = v * cos - pltpu.roll(v, 64, 1) * sin
    full = exact(jnp.where(in_a, v, 0.0), stab[...]) + local[...]
    for n in range(4):
        cx[n] = full[:, n * 128 : (n + 1) * 128]

    def final_step(c, carry):
        rows = []
        for n in range(4):
            fix = jnp.broadcast_to(cx[n, pl.ds(c, 1), :], (16, 128))
            base = pl.multiple_of(c * PAD, 8)
            rows.append(xs[pl.ds(base + 16 * n, 16), :] + fix * mf[16 * n : 16 * (n + 1), :])
        out_ref[c] = jnp.concatenate(rows, axis=0).astype(BF16)
        return carry

    lax.fori_loop(0, C, final_step, 0, unroll=2)


def local_program(consts, x, mask, w, wp, bp, win, wout, wc, cp, cb):
    vmem = pl.BlockSpec(memory_space=pltpu.VMEM)
    hbm = pl.BlockSpec(memory_space=pl.ANY)
    n_remote = 8 + 17
    return pl.pallas_call(
        kernel,
        out_shape=jax.ShapeDtypeStruct((C, TX, TY), BF16),
        in_specs=[vmem, vmem, hbm, vmem, vmem, vmem, vmem, hbm, vmem, vmem] + [vmem] * 8 + [hbm],
        out_specs=vmem,
        scratch_shapes=[
            pltpu.VMEM((C * PAD, 128), F32),
            pltpu.VMEM((TX, TY), F32),
            pltpu.VMEM((GROUPS, C, 1024), BF16),
            pltpu.VMEM((GROUPS, C, 1024), BF16),
            pltpu.VMEM((3, 2, 2048, 64), F32),
            pltpu.VMEM((GROUPS, C, 128), BF16),
            pltpu.VMEM((2, C, 128), F32),
            pltpu.VMEM((3, C, 128), F32),
            pltpu.VMEM((2, C, 128), F32),
            pltpu.VMEM((2, 2, C, 128), F32),
            pltpu.VMEM((2, 2, 32, 128), F32),
            pltpu.VMEM((2, 2, 32, 128), F32),
            pltpu.VMEM((3, 32, 128), F32),
            pltpu.VMEM((17, 32, 128), F32),
            pltpu.VMEM((C, 512), F32),
            pltpu.VMEM((4, C, 128), F32),
            pltpu.VMEM((2, 128), F32),
            pltpu.SemaphoreType.DMA((4,)),
            pltpu.SemaphoreType.DMA((n_remote,)),
            pltpu.SemaphoreType.DMA((n_remote,)),
        ],
        compiler_params=pltpu.CompilerParams(
            collective_id=0, has_side_effects=True, vmem_limit_bytes=48 * 1024 * 1024
        ),
        name="ocean",
    )(
        x, mask, w.reshape(2, 2, 2048, 64), wp, bp, win, wout, wc.reshape(2, 2048, 64), cp, cb.reshape(1, 64),
        consts["table"], consts["basis"], consts["pool"], consts["rot"], consts["ctab"], consts["stab"],
        consts["spread"], consts["place"], consts["dev"],
    )


def solution(mesh):
    consts = constants()

    def body(*args):
        return local_program({k: jnp.asarray(v) for k, v in consts.items()}, *args)

    placed = (P(None, "tile", "grp"), P("tile", "grp"), P(), P(), P(), P(), P(), P(), P(), P())
    return jax.shard_map(body, mesh=mesh, in_specs=placed, out_specs=P(None, "tile", "grp"), check_vma=False)
```

```python
import functools
import math

import jax
import jax.numpy as jnp
import numpy as np
from jax import lax
from jax.experimental import pallas as pl
from jax.experimental.pallas import tpu as pltpu
from jax.sharding import PartitionSpec as P

MESH = pl.DeviceIdType.MESH
F32 = jnp.float32
BF16 = jnp.bfloat16
PRECISE = lax.Precision.HIGHEST

C = 64
F = 128
TX = 64
TY = 128
L1 = 192
L2 = 256
NT = 64
NG = 4
PAD = 72
GROUPS = 8
GELU0 = math.sqrt(2.0 / math.pi)
GELU1 = GELU0 * 0.044715


def lane_numbers():
    lane = np.arange(128)
    ri, half, k = lane // 64, (lane // 32) % 2, lane % 32
    i, j = k // 4, k % 4
    kappa = np.where(i < 4, i, i - 8)
    return ri, half, kappa, j


def constants():
    ri, half, kappa, j = lane_numbers()
    two_pi = 2.0 * np.pi
    cell = np.arange(1024)
    b, q = cell // 128, cell % 128

    phi = two_pi * (b[:, None] * kappa / L1 + (q % 64)[:, None] * j / L2)
    table = np.where(ri == 0, np.cos(phi), -np.sin(phi)) * ((q // 64)[:, None] == half)

    rows = np.arange(64)
    ri_r, k_r = rows // 32, rows % 32
    i_r, j_r = k_r // 4, k_r % 4
    kap_r = np.where(i_r < 4, i_r, i_r - 8)
    phi = two_pi * (kap_r[:, None] * (64 + b) / L1 + j_r[:, None] * (64 + q) / L2)
    basis = np.where(ri_r[:, None] == 0, np.cos(phi), -np.sin(phi))

    pool = ((np.arange(128) % 8)[None, :] == (q // 16)[:, None]) & (np.arange(128) < 32)[None, :]

    def forward(theta):
        return np.cos(theta), np.where(ri == 0, 1.0, -1.0) * np.sin(theta)

    weight = np.where(j == 0, 1.0, 2.0)
    rot = []
    for a in range(GROUPS):
        rot += list(forward(two_pi * kappa * a / 24))
    for rho in range(3):
        rot += list(forward(two_pi * kappa * rho / 3))
    rot += list(forward(two_pi * j * np.where(half == 0, 1, 2) / 4))
    rot += list(forward(two_pi * j * 3 / 4))
    for a in range(GROUPS):
        cos, sin = forward(two_pi * kappa * a / 24)
        rot += [0.5 * cos * weight / (L1 * L2), -0.5 * sin * weight / (L1 * L2)]
    rot = np.stack(rot)
    rot = np.concatenate([rot, np.zeros((48 - rot.shape[0], 128))])

    small = np.arange(128)
    br, bq = small // 8, small % 8
    theta = two_pi * (br[:, None] * kappa / 256 + bq[:, None] * j / 32)
    ctab = np.where(ri == 0, np.cos(theta), -np.sin(theta)) * (small < 32)[:, None]
    wide = np.arange(512)
    wr, wq = wide // 128, (wide % 128) // 16
    theta = two_pi * (kappa[:, None] * wr / 256 + j[:, None] * wq / 32)
    stab = np.where(ri[:, None] == 0, np.cos(theta), -np.sin(theta)) * weight[:, None] / (256 * 32)
    stab = stab * (half == 0)[:, None]
    spread = ((br[:, None] == wr) & (bq[:, None] == wq) & (small < 32)[:, None])

    place = np.zeros((64, 128))
    for c in range(64):
        place[c, (32 + c) if c < 32 else (64 + c)] = 1.0

    dev = np.zeros((NT * NG, 2, 128))
    for t in range(NT):
        for g in range(NG):
            dev[t * NG + g, 0], dev[t * NG + g, 1] = forward(two_pi * ((kappa * t % 64) / 64 + (j * g % 4) / 4))
    late = np.concatenate([ctab, stab, spread], axis=1)
    return dict(
        table=table.astype(BF16),
        basis=basis.astype(BF16),
        pool=pool.astype(np.float32).astype(BF16),
        place=place.astype(BF16),
        rot=rot.astype(np.float32),
        late=late.astype(np.float32),
        dev=dev.astype(np.float32),
    )


ROW3, OWN, REC, SYN = 16, 22, 24, 26


def gelu_of_double(h):
    return h + h * jnp.tanh(h * (2.0 * GELU0 + 8.0 * GELU1 * (h * h)))


def dot(a, b):
    return jnp.dot(a, b, preferred_element_type=F32)


def exact(a, b):
    return jnp.dot(a, b, precision=PRECISE, preferred_element_type=F32)


XCHUNKS = 4
UNROLL = 3


def kernel(
    x_hbm, mask_hbm, w_hbm, wp_hbm, bp_hbm, win_hbm, wout_hbm, wc_hbm, cp_hbm, cb_hbm,
    table_hbm, basis_hbm, pool_hbm, place_hbm, rot_hbm, late_hbm, dev_hbm,
    out_ref,
    x_ref, mask_ref, wv, wp_ref, bp_ref, wint_ref, wout_ref, cp_ref, cb_ref,
    table, basis, pool, place, rot, late, devv,
    xs, mf, fa, fb, wb, lhs, wpad, win, bias, pre_s, hid_s, esend, erecv, csend, crecv, local, cx,
    lsem, ssem, rsem,
):
    t = lax.axis_index("tile")
    g = lax.axis_index("grp")

    count = [0]

    def load(src, dst):
        copy = pltpu.make_async_copy(src, dst, lsem.at[count[0]])
        count[0] += 1
        copy.start()
        return copy

    step_c = C // XCHUNKS
    get_mask = load(mask_hbm, mask_ref)
    get_x = [load(x_hbm.at[pl.ds(n * step_c, step_c)], x_ref.at[pl.ds(n * step_c, step_c)]) for n in range(XCHUNKS)]
    get_table = load(table_hbm, table)
    get_rot = load(rot_hbm, rot)
    get_w = [load(w_hbm.at[0], wv.at[0])]
    get_small = [
        load(wp_hbm, wp_ref), load(bp_hbm, bp_ref), load(win_hbm, wint_ref), load(wout_hbm, wout_ref),
        load(cp_hbm, cp_ref), load(cb_hbm, cb_ref), load(place_hbm, place), load(basis_hbm, basis),
    ]
    get_w.append(load(w_hbm.at[1], wv.at[1]))
    get_w.append(load(wc_hbm, wv.at[2]))
    get_late = [load(pool_hbm, pool), load(late_hbm, late), load(dev_hbm.at[t * NG + g], devv)]

    def at(tile, grp):
        return {"tile": tile, "grp": grp}

    around = []
    for dt in (-1, 0, 1):
        for dg in (-1, 0, 1):
            if dt or dg:
                around.append((dt, dg, at(lax.rem(t + (dt + NT), NT), lax.rem(g + (dg + NG), NG))))
    yc, xc, zlo = lax.rem(t, 8), lax.div(t, 16), lax.rem(lax.div(t, 8), 2)
    zc = 2 * g + zlo
    plane = []
    for dx in range(4):
        row = lax.rem(xc + dx, 4) * 16 + zlo * 8
        plane += [at(row + lax.rem(yc + d, 8), g) for d in range(8) if dx or d]
    along_z = []
    for d in range(1, 8):
        z = lax.rem(zc + d, 8)
        along_z.append(at(xc * 16 + lax.rem(z, 2) * 8 + yc, lax.div(z, 2)))

    barrier = pltpu.get_barrier_semaphore()
    partners = [device for _, _, device in around] + plane + along_z
    for partner in partners:
        pl.semaphore_signal(barrier, inc=1, device_id=partner, device_id_type=MESH)

    lane = lax.broadcasted_iota(jnp.int32, (64, 128), 1)
    mode = lane % 32
    in_a = (lane // 32) % 2 == 0
    in_a32 = in_a[:32]
    re_sign = jnp.where(lane < 64, -1.0, 1.0).astype(F32)

    def turned(v, row):
        return v * rot[row : row + 1, :] + pltpu.roll(v, 64, 1) * rot[row + 1 : row + 2, :]

    get_mask.wait()
    mf[...] = mask_ref[...].astype(F32)

    def mask_step(c, carry):
        xs[pl.ds(pl.multiple_of(c * PAD, 8), 64), :] = jnp.where(mask_ref[...] > 0, x_ref[c].astype(F32), 0.0)
        return carry

    for n in range(XCHUNKS):
        get_x[n].wait()
        lax.fori_loop(n * step_c, (n + 1) * step_c, mask_step, 0, unroll=4)

    def group_step(a, carry):
        for b in range(8):
            fa[a + 1, :, b * 128 : (b + 1) * 128] = xs[pl.ds(8 * a + b, 64, stride=PAD), :].astype(BF16)
        return carry

    lax.fori_loop(0, GROUPS, group_step, 0)

    get_table.wait()
    get_rot.wait()
    parts = dot(fa[1:].reshape(512, 1024), table[...])
    total = turned(parts[:64], 0)
    for a in range(1, GROUPS):
        total = total + turned(parts[a * 64 : (a + 1) * 64], 2 * a)

    def remote(src, dst, number, device):
        return pltpu.make_async_remote_copy(
            src_ref=src, dst_ref=dst, send_sem=ssem.at[number], recv_sem=rsem.at[number],
            device_id=device, device_id_type=MESH,
        )

    def prepare(l):
        get_w[l].wait()

        def prepare_step(n, carry):
            rows = pl.ds(pl.multiple_of(n * 256, 256), 256)
            late_rows = pl.ds(pl.multiple_of(1024 + n * 256, 256), 256)
            wb[l, rows, :128] = jnp.concatenate([wv[l, 0, rows, :], wv[l, 1, rows, :]], axis=1).astype(BF16)
            wb[l, rows, 128:] = jnp.concatenate([wv[l, 0, late_rows, :], wv[l, 1, late_rows, :]], axis=1).astype(BF16)
            return carry

        lax.fori_loop(0, 4, prepare_step, 0)

    def exchange(l, total, beside):
        whole = turned(total, OWN)
        whole = whole + pltpu.roll(whole, 96, 1)
        packed = jnp.where(in_a32, whole[:32], pltpu.roll(whole[32:], 32, 1))
        esend[l, 1] = packed.astype(BF16)
        esend[l, 0] = jnp.where(in_a32, total[:32], pltpu.roll(total[32:], 32, 1)).astype(BF16)
        esend[l, 2] = jnp.where(in_a32, pltpu.roll(total[:32], 96, 1), total[32:]).astype(BF16)
        sends = []
        for n, (dt, dg, device) in enumerate(around):
            sends.append(remote(esend.at[l, dg + 1], erecv.at[l, 1 - dt, 1 - dg], 8 * l + n, device))
        for s in sends:
            s.start()
        beside()
        for s in sends:
            s.wait()
        rows = (t > 0, None, t < NT - 1)
        total = None
        for r in range(3):
            from_left = jnp.where(g > 0, erecv[l, r, 0].astype(F32), 0.0)
            from_right = jnp.where(g < NG - 1, erecv[l, r, 2].astype(F32), 0.0)
            middle = packed if r == 1 else erecv[l, r, 1].astype(F32)
            one = turned(middle + from_left + turned(from_right, REC), ROW3 + 2 * r)
            if rows[r] is not None:
                one = jnp.where(rows[r], one, 0.0)
            total = one if total is None else total + one
        return jnp.concatenate([total, pltpu.roll(total, 96, 1)], axis=0)

    def mix(l, u):
        sides = jnp.concatenate([u, pltpu.roll(u, 64, 1) * re_sign], axis=0).astype(BF16)
        none = jnp.zeros_like(sides)
        both = jnp.concatenate(
            [jnp.concatenate([sides, none], axis=1), jnp.concatenate([none, sides], axis=1)], axis=0
        )
        acc = jnp.zeros((64, 128), F32)
        for block in range(4):
            o = dot(wb[l, block * 256 : (block + 1) * 256, :], both)
            for n in range(4):
                k = block * 4 + n
                acc = jnp.where(mode == k, o[n * 64 : (n + 1) * 64, :128], acc)
                acc = jnp.where(mode == k + 16, o[n * 64 : (n + 1) * 64, 128:], acc)
        return acc

    def layer(l, src, dst, v, matrix, finish):
        swapped = pltpu.roll(v, 64, 1)
        for a in range(GROUPS):
            lhs[a] = jnp.where(in_a, v * rot[SYN + 2 * a : SYN + 2 * a + 1, :] + swapped * rot[SYN + 2 * a + 1 : SYN + 2 * a + 2, :], wpad[l]).astype(BF16)
        shift = jnp.concatenate([bias[l], bias[l]], axis=1)

        def first(a, cols):
            rhs = jnp.concatenate(
                [basis[:32, cols], src[a + 1, :32, cols], basis[32:, cols], src[a + 1, 32:, cols]], axis=0
            )
            return dot(lhs[a], rhs)

        def second(pre):
            return dot(win[l], gelu_of_double(pre + shift).astype(BF16))

        def third(hid, row):
            sea = jnp.concatenate([mf[pl.ds(row, 1), :], mf[pl.ds(row + 1, 1), :]], axis=1)
            return (dot(wout_ref[l], gelu_of_double(hid).astype(BF16)) * sea).astype(BF16)

        def step(i, total):
            for inner in range(UNROLL):
                a = UNROLL * i + inner
                part = None
                for n in range(4):
                    m = (n + 2) % 4
                    cols = slice(n * 256, (n + 1) * 256)
                    pre_s[n] = first(jnp.minimum(a, GROUPS - 1), cols)
                    hid_s[m] = second(pre_s[m])
                    new = third(hid_s[n], jnp.maximum(8 * a - 8 + 2 * n, 0))
                    dst[a, :, cols] = new
                    piece = dot(new, matrix[cols, :])
                    part = piece if n == 0 else part + piece
                total = finish(a - 1, part, total)
            return total

        return lax.fori_loop(0, (GROUPS + 1) // UNROLL, step, jnp.zeros((64, 128), F32))

    def analysis(a, part, total):
        at_a = 2 * jnp.maximum(a, 0)
        part = part * rot[pl.ds(at_a, 1), :] + pltpu.roll(part, 64, 1) * rot[pl.ds(at_a + 1, 1), :]
        return total + jnp.where(a >= 0, part, 0.0)

    for copy in get_small:
        copy.wait()
    eye = lax.broadcasted_iota(jnp.int32, (64, 64), 0) == lax.broadcasted_iota(jnp.int32, (64, 64), 1)

    def column(row):
        return jnp.broadcast_to(jnp.sum(jnp.where(eye, row, 0.0), axis=1, keepdims=True), (64, 128))

    for l in range(2):
        wpad[l] = 0.5 * dot(wp_ref[l], place[...])
        win[l] = (0.5 * wint_ref[l].astype(F32)).T.astype(BF16)
        bias[l] = 0.5 * column(bp_ref[l : l + 1, :])
    bias[2] = column(cb_ref[...])

    pl.semaphore_wait(barrier, len(partners))
    u = exchange(0, total, lambda: prepare(0))
    v = mix(0, u)
    total = layer(0, fa, fb, v, table, analysis)
    u = exchange(1, total, lambda: prepare(1))
    v = mix(1, u)
    for copy in get_late:
        copy.wait()

    def pooled(a, part, total):
        return total + jnp.where((lane // 8 == a // 2) & (a >= 0), part, 0.0)

    coarse = layer(1, fb, fa, v, pool, pooled) * (1.0 / 256.0)

    cos, sin = devv[0:1, :], devv[1:2, :]
    part = exact(coarse, late[:, :128])
    part = part * cos + pltpu.roll(part, 64, 1) * sin
    acc = jnp.where(in_a32, part[:32], part[32:])
    number, slot = 16, 0
    for stage, peers in enumerate((plane, along_z)):
        csend[stage] = acc.astype(BF16)
        sends = []
        for peer in peers:
            sends.append(remote(csend.at[stage], crecv.at[slot], number, peer))
            number, slot = number + 1, slot + 1
        for s in sends:
            s.start()
        if stage == 0:
            local[...] = exact(cp_ref[...], exact(coarse, late[:, 640:])) + jnp.concatenate([bias[2]] * 4, axis=1)
            prepare(2)
        else:
            def back_step(a, carry):
                for b in range(8):
                    xs[pl.ds(8 * a + b, 64, stride=PAD), :] = fa[a + 1, :, b * 128 : (b + 1) * 128].astype(F32)
                return carry

            lax.fori_loop(0, GROUPS, back_step, 0)
        for s in sends:
            s.wait()
        for n in range(slot - len(peers), slot):
            acc = acc + crecv[n].astype(F32)
    u = jnp.concatenate([acc, pltpu.roll(acc, 96, 1)], axis=0)
    v = mix(2, u)
    v = v * cos - pltpu.roll(v, 64, 1) * sin
    full = exact(jnp.where(in_a, v, 0.0), late[:, 128:640]) + local[...]
    for n in range(4):
        cx[n] = full[:, n * 128 : (n + 1) * 128]

    def final_step(c, carry):
        rows = []
        for n in range(4):
            fix = jnp.broadcast_to(cx[n, pl.ds(c, 1), :], (16, 128))
            base = pl.multiple_of(c * PAD, 8)
            rows.append(xs[pl.ds(base + 16 * n, 16), :] + fix * mf[16 * n : 16 * (n + 1), :])
        out_ref[c] = jnp.concatenate(rows, axis=0).astype(BF16)
        return carry

    lax.fori_loop(0, C, final_step, 0, unroll=4)


def local_program(consts, x, mask, w, wp, bp, win, wout, wc, cp, cb):
    hbm = pl.BlockSpec(memory_space=pltpu.HBM)
    n_remote = 16 + 38
    names = ["table", "basis", "pool", "place", "rot", "late", "dev"]
    return pl.pallas_call(
        kernel,
        out_shape=jax.ShapeDtypeStruct((C, TX, TY), BF16),
        in_specs=[hbm] * (10 + len(names)),
        out_specs=pl.BlockSpec(memory_space=pltpu.VMEM),
        scratch_shapes=[
            pltpu.VMEM((C, TX, TY), BF16),
            pltpu.VMEM((TX, TY), jnp.int32),
            pltpu.VMEM((3, 2, 2048, 64), F32),
            pltpu.VMEM((2, C, C), BF16),
            pltpu.VMEM((2, C), F32),
            pltpu.VMEM((2, C, F), BF16),
            pltpu.VMEM((2, C, F), BF16),
            pltpu.VMEM((C, C), F32),
            pltpu.VMEM((1, C), F32),
            pltpu.VMEM((1024, 128), BF16),
            pltpu.VMEM((64, 1024), BF16),
            pltpu.VMEM((1024, 128), BF16),
            pltpu.VMEM((64, 128), BF16),
            pltpu.VMEM((48, 128), F32),
            pltpu.VMEM((128, 1152), F32),
            pltpu.VMEM((2, 128), F32),
            pltpu.VMEM((C * PAD, 128), F32),
            pltpu.VMEM((TX, TY), F32),
            pltpu.VMEM((GROUPS + 1, C, 1024), BF16),
            pltpu.VMEM((GROUPS + 1, C, 1024), BF16),
            pltpu.VMEM((3, 1024, 256), BF16),
            pltpu.VMEM((GROUPS, C, 128), BF16),
            pltpu.VMEM((2, C, 128), F32),
            pltpu.VMEM((2, F, C), BF16),
            pltpu.VMEM((3, C, 128), F32),
            pltpu.VMEM((4, C, 256), F32),
            pltpu.VMEM((4, F, 256), F32),
            pltpu.VMEM((2, 3, 32, 128), BF16),
            pltpu.VMEM((2, 3, 3, 32, 128), BF16),
            pltpu.VMEM((2, 32, 128), BF16),
            pltpu.VMEM((38, 32, 128), BF16),
            pltpu.VMEM((C, 512), F32),
            pltpu.VMEM((4, C, 128), F32),
            pltpu.SemaphoreType.DMA((22,)),
            pltpu.SemaphoreType.DMA((n_remote,)),
            pltpu.SemaphoreType.DMA((n_remote,)),
        ],
        compiler_params=pltpu.CompilerParams(
            collective_id=0, has_side_effects=True, vmem_limit_bytes=48000 * 1024
        ),
        name="ocean",
    )(
        *[
            pltpu.with_memory_space_constraint(v, pltpu.HBM)
            for v in (
                x, mask, w.reshape(2, 2, 2048, 64), wp, bp, jnp.swapaxes(win, 1, 2), wout,
                wc.reshape(2, 2048, 64), cp, cb.reshape(1, 64), *[consts[name] for name in names],
            )
        ]
    )


def solution(mesh):
    consts = constants()

    def body(*args):
        return local_program({k: jnp.asarray(v) for k, v in consts.items()}, *args)

    placed = (P(None, "tile", "grp"), P("tile", "grp"), P(), P(), P(), P(), P(), P(), P(), P())
    return jax.shard_map(body, mesh=mesh, in_specs=placed, out_specs=P(None, "tile", "grp"), check_vma=False)
```

```python
import functools
import math

import jax
import jax.numpy as jnp
import numpy as np
from jax import lax
from jax.experimental import pallas as pl
from jax.experimental.pallas import tpu as pltpu
from jax.sharding import PartitionSpec as P

MESH = pl.DeviceIdType.MESH
F32 = jnp.float32
BF16 = jnp.bfloat16
PRECISE = lax.Precision.HIGHEST

C = 64
F = 128
TX = 64
TY = 128
L1 = 192
L2 = 256
NT = 64
NG = 4
PAD = 72
GROUPS = 8
GELU0 = math.sqrt(2.0 / math.pi)
GELU1 = GELU0 * 0.044715


def lane_numbers():
    lane = np.arange(128)
    ri, half, k = lane // 64, (lane // 32) % 2, lane % 32
    i, j = k // 4, k % 4
    kappa = np.where(i < 4, i, i - 8)
    return ri, half, kappa, j


def constants():
    ri, half, kappa, j = lane_numbers()
    two_pi = 2.0 * np.pi
    cell = np.arange(1024)
    b, q = cell // 128, cell % 128

    phi = two_pi * (b[:, None] * kappa / L1 + (q % 64)[:, None] * j / L2)
    table = np.where(ri == 0, np.cos(phi), -np.sin(phi)) * ((q // 64)[:, None] == half)

    rows = np.arange(64)
    ri_r, k_r = rows // 32, rows % 32
    i_r, j_r = k_r // 4, k_r % 4
    kap_r = np.where(i_r < 4, i_r, i_r - 8)
    phi = two_pi * (kap_r[:, None] * (64 + b) / L1 + j_r[:, None] * (64 + q) / L2)
    basis = np.where(ri_r[:, None] == 0, np.cos(phi), -np.sin(phi))
    basis[32] = 1.0
    basis = basis.reshape(64, 8, 128).transpose(1, 0, 2)

    pool = ((np.arange(128) % 8)[None, :] == (q // 16)[:, None]) & (np.arange(128) < 32)[None, :]

    def forward(theta):
        return np.cos(theta), np.where(ri == 0, 1.0, -1.0) * np.sin(theta)

    weight = np.where(j == 0, 1.0, 2.0)
    rot = []
    for a in range(GROUPS):
        rot += list(forward(two_pi * kappa * a / 24))
    for rho in range(3):
        rot += list(forward(two_pi * kappa * rho / 3))
    rot += list(forward(two_pi * j * np.where(half == 0, 1, 2) / 4))
    rot += list(forward(two_pi * j * 3 / 4))
    for a in range(GROUPS):
        cos, sin = forward(two_pi * kappa * a / 24)
        keep = 0.5 * weight / (L1 * L2) * (half == 0) * (np.arange(128) != 64)
        rot += [keep * cos, -keep * sin]
    rot = np.stack(rot)
    rot = np.concatenate([rot, np.zeros((48 - rot.shape[0], 128))])

    small = np.arange(128)
    br, bq = small // 8, small % 8
    theta = two_pi * (br[:, None] * kappa / 256 + bq[:, None] * j / 32)
    ctab = np.where(ri == 0, np.cos(theta), -np.sin(theta)) * (small < 32)[:, None]
    wide = np.arange(512)
    wr, wq = wide // 128, (wide % 128) // 16
    theta = two_pi * (kappa[:, None] * wr / 256 + j[:, None] * wq / 32)
    stab = np.where(ri[:, None] == 0, np.cos(theta), -np.sin(theta)) * weight[:, None] / (256 * 32)
    stab = stab * (half == 0)[:, None]
    spread = ((br[:, None] == wr) & (bq[:, None] == wq) & (small < 32)[:, None])

    place = np.zeros((64, 128))
    for c in range(64):
        place[c, (32 + c) if c < 32 else (64 + c)] = 1.0

    dev = np.zeros((NT * NG, 2, 128))
    for t in range(NT):
        for g in range(NG):
            dev[t * NG + g, 0], dev[t * NG + g, 1] = forward(two_pi * ((kappa * t % 64) / 64 + (j * g % 4) / 4))
    high = ctab.astype(np.float32).astype(BF16).astype(np.float64)
    ctab3 = np.concatenate([high[:32], high[:32], (ctab - high)[:32], np.zeros((32, 128))])
    sums = np.concatenate([np.concatenate([stab] * 2, axis=0), np.concatenate([ctab3, np.zeros((128, 128))])], axis=1)
    return dict(
        table=table.astype(BF16),
        basis=basis.astype(BF16),
        pool=pool.astype(np.float32).astype(BF16),
        place=place.astype(BF16),
        rot=rot.astype(np.float32),
        sums=sums.astype(np.float32).astype(BF16),
        late=spread.astype(np.float32),
        dev=dev.astype(np.float32),
    )


ROW3, OWN, REC, SYN = 16, 22, 24, 26


def gelu_of_double(h):
    return h + h * jnp.tanh(h * (2.0 * GELU0 + 8.0 * GELU1 * (h * h)))


def dot(a, b):
    return jnp.dot(a, b, preferred_element_type=F32)


def exact(a, b):
    return jnp.dot(a, b, precision=PRECISE, preferred_element_type=F32)


XCHUNKS = 4
UNROLL = 9


def kernel(
    x_hbm, mask_hbm, w_hbm, wp_hbm, bp_hbm, win_hbm, wout_hbm, wc_hbm, cp_hbm, cb_hbm,
    table_hbm, basis_hbm, pool_hbm, place_hbm, rot_hbm, sums_hbm, late_hbm, dev_hbm,
    out_ref,
    x_ref, mask_ref, wv, wp_ref, bp_ref, wint_ref, wout_ref, cp_ref, cb_ref,
    table, basis, pool, place, rot, sums, late, devv,
    xs, mf, fa, fb, wb, lhs, wpad, win, bias, pre_s, hid_s, parts_s, esend, erecv, csend, crecv, local, cx,
    lsem, ssem, rsem,
):
    t = lax.axis_index("tile")
    g = lax.axis_index("grp")

    count = [0]

    def load(src, dst):
        copy = pltpu.make_async_copy(src, dst, lsem.at[count[0]])
        count[0] += 1
        copy.start()
        return copy

    step_c = C // XCHUNKS
    get_mask = load(mask_hbm, mask_ref)
    get_x = [load(x_hbm.at[pl.ds(n * step_c, step_c)], x_ref.at[pl.ds(n * step_c, step_c)]) for n in range(XCHUNKS)]
    def at(tile, grp):
        return {"tile": tile, "grp": grp}

    row_there = {-1: t > 0, 1: t < NT - 1}
    column_there = {-1: g > 0, 1: g < NG - 1}

    def there(dt, dg):
        if dt and dg:
            return row_there[dt] & column_there[dg]
        return row_there[dt] if dt else column_there[dg]

    around = []
    for dt, dg in ((-1, -1), (-1, 1), (1, -1), (1, 1), (-1, 0), (1, 0), (0, -1), (0, 1)):
        around.append((dt, dg, at(lax.rem(t + (dt + NT), NT), lax.rem(g + (dg + NG), NG))))
    yc, xc, zlo = lax.rem(t, 8), lax.div(t, 16), lax.rem(lax.div(t, 8), 2)
    zc = 2 * g + zlo
    plane = []
    for dx in range(4):
        row = lax.rem(xc + dx, 4) * 16 + zlo * 8
        plane += [at(row + lax.rem(yc + d, 8), g) for d in range(8) if dx or d]
    along_z = []
    for d in range(1, 8):
        z = lax.rem(zc + d, 8)
        along_z.append(at(xc * 16 + lax.rem(z, 2) * 8 + yc, lax.div(z, 2)))

    barrier = pltpu.get_barrier_semaphore()
    expected = jnp.int32(len(plane) + len(along_z))
    for dt, dg, device in around:
        expected = expected + there(dt, dg).astype(jnp.int32)

        @pl.when(there(dt, dg))
        def greet(device=device):
            pl.semaphore_signal(barrier, inc=1, device_id=device, device_id_type=MESH)

    for partner in along_z + plane:
        pl.semaphore_signal(barrier, inc=1, device_id=partner, device_id_type=MESH)

    get_table = load(table_hbm, table)
    get_rot = load(rot_hbm, rot)
    get_w = [load(w_hbm.at[0], wv.at[0])]
    get_small = [
        load(wp_hbm, wp_ref), load(bp_hbm, bp_ref), load(win_hbm, wint_ref), load(wout_hbm, wout_ref),
        load(cp_hbm, cp_ref), load(cb_hbm, cb_ref), load(place_hbm, place), load(basis_hbm, basis),
    ]
    get_w.append(load(w_hbm.at[1], wv.at[1]))
    get_w.append(load(wc_hbm, wv.at[2]))
    get_late = [load(pool_hbm, pool), load(sums_hbm, sums), load(late_hbm, late), load(dev_hbm.at[t * NG + g], devv)]

    lane = lax.broadcasted_iota(jnp.int32, (64, 128), 1)
    mode = lane % 32
    in_a = (lane // 32) % 2 == 0
    in_a32 = in_a[:32]
    re_sign = jnp.where(lane < 64, -1.0, 1.0).astype(F32)

    def turned(v, row):
        return v * rot[row : row + 1, :] + pltpu.roll(v, 64, 1) * rot[row + 1 : row + 2, :]

    get_mask.wait()
    mf[...] = mask_ref[...].astype(F32)

    def mask_step(c, carry):
        xs[pl.ds(pl.multiple_of(c * PAD, 8), 64), :] = jnp.where(mask_ref[...] > 0, x_ref[c].astype(F32), 0.0)
        return carry

    for n in range(XCHUNKS):
        get_x[n].wait()
        lax.fori_loop(n * step_c, (n + 1) * step_c, mask_step, 0, unroll=4)

    def group_step(a, carry):
        for b in range(8):
            fa[a + 1, b] = xs[pl.ds(8 * a + b, 64, stride=PAD), :].astype(BF16)
        return carry

    lax.fori_loop(0, GROUPS, group_step, 0)

    get_table.wait()
    get_rot.wait()
    parts = dot(jnp.concatenate([fa[1:, b].reshape(512, 128) for b in range(8)], axis=1), table[...])
    total = turned(parts[:64], 0)
    for a in range(1, GROUPS):
        total = total + turned(parts[a * 64 : (a + 1) * 64], 2 * a)

    def remote(src, dst, number, device):
        return pltpu.make_async_remote_copy(
            src_ref=src, dst_ref=dst, send_sem=ssem.at[number], recv_sem=rsem.at[number],
            device_id=device, device_id_type=MESH,
        )

    def prepare(l):
        get_w[l].wait()

        def prepare_step(n, carry):
            rows = pl.ds(pl.multiple_of(n * 256, 256), 256)
            late_rows = pl.ds(pl.multiple_of(1024 + n * 256, 256), 256)
            wb[l, rows, :128] = jnp.concatenate([wv[l, 0, rows, :], wv[l, 1, rows, :]], axis=1).astype(BF16)
            wb[l, rows, 128:] = jnp.concatenate([wv[l, 0, late_rows, :], wv[l, 1, late_rows, :]], axis=1).astype(BF16)
            return carry

        lax.fori_loop(0, 4, prepare_step, 0)

    def exchange(l, total, beside):
        whole = turned(total, OWN)
        whole = whole + pltpu.roll(whole, 96, 1)
        packed = jnp.where(in_a32, whole[:32], pltpu.roll(whole[32:], 32, 1))
        esend[l, 1] = packed.astype(BF16)
        esend[l, 0] = jnp.where(in_a32, total[:32], pltpu.roll(total[32:], 32, 1)).astype(BF16)
        esend[l, 2] = jnp.where(in_a32, pltpu.roll(total[:32], 96, 1), total[32:]).astype(BF16)
        sends = []
        for n, (dt, dg, device) in enumerate(around):
            sends.append(remote(esend.at[l, dg + 1], erecv.at[l, 1 - dt, 1 - dg], 8 * l + n, device))
        for (dt, dg, _), send in zip(around, sends):
            pl.when(there(dt, dg))(send.start)
        beside()
        for (dt, dg, _), send in zip(around, sends):
            pl.when(there(dt, dg))(send.wait_send)
            pl.when(there(-dt, -dg))(send.wait_recv)
        rows = (t > 0, None, t < NT - 1)
        total = None
        for r in range(3):
            from_left = jnp.where(g > 0, erecv[l, r, 0].astype(F32), 0.0)
            from_right = jnp.where(g < NG - 1, erecv[l, r, 2].astype(F32), 0.0)
            middle = packed if r == 1 else erecv[l, r, 1].astype(F32)
            one = turned(middle + from_left + turned(from_right, REC), ROW3 + 2 * r)
            if rows[r] is not None:
                one = jnp.where(rows[r], one, 0.0)
            total = one if total is None else total + one
        return jnp.concatenate([total, pltpu.roll(total, 96, 1)], axis=0)

    def mix(l, u):
        sides = jnp.concatenate([u, pltpu.roll(u, 64, 1) * re_sign], axis=0).astype(BF16)
        none = jnp.zeros_like(sides)
        both = jnp.concatenate(
            [jnp.concatenate([sides, none], axis=1), jnp.concatenate([none, sides], axis=1)], axis=0
        )
        acc = jnp.zeros((64, 128), F32)
        for block in range(4):
            o = dot(wb[l, block * 256 : (block + 1) * 256, :], both)
            for n in range(4):
                k = block * 4 + n
                acc = jnp.where(mode == k, o[n * 64 : (n + 1) * 64, :128], acc)
                acc = jnp.where(mode == k + 16, o[n * 64 : (n + 1) * 64, 128:], acc)
        return acc

    def layer(l, src, dst, v, matrix, finish):
        swapped = pltpu.roll(v, 64, 1)

        def synthesis(a):
            row = SYN + 2 * a
            return v * rot[row : row + 1, :] + swapped * rot[row + 1 : row + 2, :]

        fixed = wpad[l]
        whole = synthesis(0) + fixed
        rest = whole - whole.astype(BF16).astype(F32)
        fixed = fixed + jnp.where(lane == 64, pltpu.roll(rest, 64, 1), 0.0)
        for a in range(GROUPS):
            lhs[a] = (synthesis(a) + fixed).astype(BF16)

        def first(a, n):
            rhs = [
                jnp.concatenate([basis[b, :32], src[a + 1, b, :32], basis[b, 32:], src[a + 1, b, 32:]], axis=0)
                for b in (2 * n, 2 * n + 1)
            ]
            return dot(lhs[a], jnp.concatenate(rhs, axis=1))

        def second(pre):
            return dot(win[l], gelu_of_double(pre).astype(BF16))

        def third(hid, row):
            sea = [jnp.broadcast_to(mf[pl.ds(row + b, 1), :], (16, 128)).astype(BF16) for b in range(2)]
            sea = jnp.concatenate([jnp.concatenate(sea, axis=1)] * 4, axis=0)
            return dot(wout_ref[l], gelu_of_double(hid).astype(BF16)).astype(BF16) * sea

        def step(i, carry):
            for inner in range(UNROLL):
                a = UNROLL * i + inner
                for n in range(4):
                    pre_s[n] = first(jnp.minimum(a, GROUPS - 1), n)
                    new = third(hid_s[n], jnp.maximum(8 * a - 8 + 2 * n, 0))
                    hid_s[(n + 2) % 4] = second(pre_s[(n + 2) % 4])
                    dst[a, 2 * n] = new[:, :128]
                    dst[a, 2 * n + 1] = new[:, 128:]
                back = a
                parts_s[back] = dot(jnp.concatenate([dst[back, b] for b in range(8)], axis=1), matrix[...])
            return carry

        lax.fori_loop(0, (GROUPS + 1) // UNROLL, step, 0)
        return finish([parts_s[a + 1] for a in range(GROUPS)])

    def analysis(parts):
        total = turned(parts[0], 0)
        for a in range(1, GROUPS):
            total = total + turned(parts[a], 2 * a)
        return total

    for copy in get_small:
        copy.wait()
    eye = lax.broadcasted_iota(jnp.int32, (64, 64), 0) == lax.broadcasted_iota(jnp.int32, (64, 64), 1)

    def column(row):
        return jnp.broadcast_to(jnp.sum(jnp.where(eye, row, 0.0), axis=1, keepdims=True), (64, 128))

    for l in range(2):
        wpad[l] = 0.5 * dot(wp_ref[l], place[...]) + jnp.where(lane == 0, 0.5 * column(bp_ref[l : l + 1, :]), 0.0)
        win[l] = (0.5 * wint_ref[l].astype(F32)).T.astype(BF16)
    bias[...] = column(cb_ref[...])

    pl.semaphore_wait(barrier, expected)
    u = exchange(0, total, lambda: prepare(0))
    v = mix(0, u)
    total = layer(0, fa, fb, v, table, analysis)
    u = exchange(1, total, lambda: prepare(1))
    v = mix(1, u)
    for copy in get_late:
        copy.wait()

    def pooled(parts):
        total = jnp.zeros((64, 128), F32)
        for a in range(GROUPS):
            total = total + jnp.where(lane // 8 == a // 2, parts[a], 0.0)
        return total

    coarse = layer(1, fb, fa, v, pool, pooled) * (1.0 / 256.0)

    cos, sin = devv[0:1, :], devv[1:2, :]
    high = coarse.astype(BF16).astype(F32)
    split = jnp.where(lane < 32, high, pltpu.roll(coarse - high, 32, 1) + pltpu.roll(high, 64, 1))
    part = dot(split.astype(BF16), sums[:128, 512:])
    part = part * cos + pltpu.roll(part, 64, 1) * sin
    acc = jnp.where(in_a32, part[:32], part[32:])
    number, slot = 16, 0
    for stage, peers in enumerate((plane, along_z)):
        csend[stage] = acc.astype(BF16)
        sends = []
        for peer in peers:
            sends.append(remote(csend.at[stage], crecv.at[slot], number, peer))
            number, slot = number + 1, slot + 1
        for s in sends:
            s.start()
        if stage == 0:
            local[...] = exact(cp_ref[...], exact(coarse, late[...])) + jnp.concatenate([bias[...]] * 4, axis=1)
            prepare(2)
        else:
            def back_step(a, carry):
                for b in range(8):
                    xs[pl.ds(8 * a + b, 64, stride=PAD), :] = fa[a + 1, b].astype(F32)
                return carry

            lax.fori_loop(0, GROUPS, back_step, 0)
        for s in sends:
            s.wait()
        for n in range(slot - len(peers), slot):
            acc = acc + crecv[n].astype(F32)
    u = jnp.concatenate([acc, pltpu.roll(acc, 96, 1)], axis=0)
    v = mix(2, u)
    v = v * cos - pltpu.roll(v, 64, 1) * sin
    high = v.astype(BF16)
    split = jnp.concatenate([high, (v - high.astype(F32)).astype(BF16)], axis=1)
    full = dot(split, sums[:, :512]) + local[...]
    for n in range(4):
        cx[n] = full[:, n * 128 : (n + 1) * 128]

    def final_step(c, carry):
        rows = []
        for n in range(4):
            fix = jnp.broadcast_to(cx[n, pl.ds(c, 1), :], (16, 128))
            base = pl.multiple_of(c * PAD, 8)
            rows.append(xs[pl.ds(base + 16 * n, 16), :] + fix * mf[16 * n : 16 * (n + 1), :])
        out_ref[c] = jnp.concatenate(rows, axis=0).astype(BF16)
        return carry

    lax.fori_loop(0, C, final_step, 0, unroll=4)


def local_program(consts, x, mask, w, wp, bp, win, wout, wc, cp, cb):
    hbm = pl.BlockSpec(memory_space=pltpu.HBM)
    n_remote = 16 + 38
    names = ["table", "basis", "pool", "place", "rot", "sums", "late", "dev"]
    return pl.pallas_call(
        kernel,
        out_shape=jax.ShapeDtypeStruct((C, TX, TY), BF16),
        in_specs=[hbm] * (10 + len(names)),
        out_specs=pl.BlockSpec(memory_space=pltpu.VMEM),
        scratch_shapes=[
            pltpu.VMEM((C, TX, TY), BF16),
            pltpu.VMEM((TX, TY), jnp.int32),
            pltpu.VMEM((3, 2, 2048, 64), F32),
            pltpu.VMEM((2, C, C), BF16),
            pltpu.VMEM((2, C), F32),
            pltpu.VMEM((2, C, F), BF16),
            pltpu.VMEM((2, C, F), BF16),
            pltpu.VMEM((C, C), F32),
            pltpu.VMEM((1, C), F32),
            pltpu.VMEM((1024, 128), BF16),
            pltpu.VMEM((8, 64, 128), BF16),
            pltpu.VMEM((1024, 128), BF16),
            pltpu.VMEM((64, 128), BF16),
            pltpu.VMEM((48, 128), F32),
            pltpu.VMEM((256, 640), BF16),
            pltpu.VMEM((128, 512), F32),
            pltpu.VMEM((2, 128), F32),
            pltpu.VMEM((C * PAD, 128), F32),
            pltpu.VMEM((TX, TY), F32),
            pltpu.VMEM((GROUPS + 1, 8, C, 128), BF16),
            pltpu.VMEM((GROUPS + 1, 8, C, 128), BF16),
            pltpu.VMEM((3, 1024, 256), BF16),
            pltpu.VMEM((GROUPS, C, 128), BF16),
            pltpu.VMEM((2, C, 128), F32),
            pltpu.VMEM((2, F, C), BF16),
            pltpu.VMEM((C, 128), F32),
            pltpu.VMEM((4, C, 256), F32),
            pltpu.VMEM((4, F, 256), F32),
            pltpu.VMEM((GROUPS + 1, C, 128), F32),
            pltpu.VMEM((2, 3, 32, 128), BF16),
            pltpu.VMEM((2, 3, 3, 32, 128), BF16),
            pltpu.VMEM((2, 32, 128), BF16),
            pltpu.VMEM((38, 32, 128), BF16),
            pltpu.VMEM((C, 512), F32),
            pltpu.VMEM((4, C, 128), F32),
            pltpu.SemaphoreType.DMA((24,)),
            pltpu.SemaphoreType.DMA((n_remote,)),
            pltpu.SemaphoreType.DMA((n_remote,)),
        ],
        compiler_params=pltpu.CompilerParams(
            collective_id=0, has_side_effects=True, vmem_limit_bytes=48000 * 1024
        ),
        name="ocean",
    )(
        *[
            pltpu.with_memory_space_constraint(v, pltpu.HBM)
            for v in (
                x, mask, w.reshape(2, 2, 2048, 64), wp, bp, jnp.swapaxes(win, 1, 2), wout,
                wc.reshape(2, 2048, 64), cp, cb.reshape(1, 64), *[consts[name] for name in names],
            )
        ]
    )


def solution(mesh):
    consts = constants()

    def body(*args):
        return local_program({k: jnp.asarray(v) for k, v in consts.items()}, *args)

    placed = (P(None, "tile", "grp"), P("tile", "grp"), P(), P(), P(), P(), P(), P(), P(), P())
    return jax.shard_map(body, mesh=mesh, in_specs=placed, out_specs=P(None, "tile", "grp"), check_vma=False)
```

```python
import functools
import math

import jax
import jax.numpy as jnp
import numpy as np
from jax import lax
from jax.experimental import pallas as pl
from jax.experimental.pallas import tpu as pltpu
from jax.sharding import PartitionSpec as P

MESH = pl.DeviceIdType.MESH
F32 = jnp.float32
BF16 = jnp.bfloat16
PRECISE = lax.Precision.HIGHEST

C = 64
F = 128
TX = 64
TY = 128
L1 = 192
L2 = 256
NT = 64
NG = 4
PAD = 72
GROUPS = 8
GELU0 = math.sqrt(2.0 / math.pi)
GELU1 = GELU0 * 0.044715


def lane_numbers():
    lane = np.arange(128)
    ri, half, k = lane // 64, (lane // 32) % 2, lane % 32
    i, j = k // 4, k % 4
    kappa = np.where(i < 4, i, i - 8)
    return ri, half, kappa, j


def constants():
    ri, half, kappa, j = lane_numbers()
    two_pi = 2.0 * np.pi
    cell = np.arange(1024)
    b, q = cell // 128, cell % 128

    phi = two_pi * (b[:, None] * kappa / L1 + (q % 64)[:, None] * j / L2)
    table = np.where(ri == 0, np.cos(phi), -np.sin(phi)) * ((q // 64)[:, None] == half)

    rows = np.arange(64)
    ri_r, k_r = rows // 32, rows % 32
    i_r, j_r = k_r // 4, k_r % 4
    kap_r = np.where(i_r < 4, i_r, i_r - 8)
    phi = two_pi * (kap_r[:, None] * (64 + b) / L1 + j_r[:, None] * (64 + q) / L2)
    basis = np.where(ri_r[:, None] == 0, np.cos(phi), -np.sin(phi))
    basis[32] = 1.0
    basis = basis.reshape(64, 8, 128).transpose(1, 0, 2)

    pool = ((np.arange(128) % 8)[None, :] == (q // 16)[:, None]) & (np.arange(128) < 32)[None, :]

    def forward(theta):
        return np.cos(theta), np.where(ri == 0, 1.0, -1.0) * np.sin(theta)

    weight = np.where(j == 0, 1.0, 2.0)
    rot = []
    for a in range(GROUPS):
        rot += list(forward(two_pi * kappa * a / 24))
    for rho in range(3):
        rot += list(forward(two_pi * kappa * rho / 3))
    rot += list(forward(two_pi * j * np.where(half == 0, 1, 2) / 4))
    rot += list(forward(two_pi * j * 3 / 4))
    for a in range(GROUPS):
        cos, sin = forward(two_pi * kappa * a / 24)
        keep = 0.5 * weight / (L1 * L2) * (half == 0) * (np.arange(128) != 64)
        rot += [keep * cos, -keep * sin]
    rot = np.stack(rot)
    rot = np.concatenate([rot, np.zeros((48 - rot.shape[0], 128))])

    small = np.arange(128)
    br, bq = small // 8, small % 8
    theta = two_pi * (br[:, None] * kappa / 256 + bq[:, None] * j / 32)
    ctab = np.where(ri == 0, np.cos(theta), -np.sin(theta)) * (small < 32)[:, None]
    wide = np.arange(512)
    wr, wq = wide // 128, (wide % 128) // 16
    theta = two_pi * (kappa[:, None] * wr / 256 + j[:, None] * wq / 32)
    stab = np.where(ri[:, None] == 0, np.cos(theta), -np.sin(theta)) * weight[:, None] / (256 * 32)
    stab = stab * (half == 0)[:, None]
    spread = ((br[:, None] == wr) & (bq[:, None] == wq) & (small < 32)[:, None])

    place = np.zeros((64, 128))
    for c in range(64):
        place[c, (32 + c) if c < 32 else (64 + c)] = 1.0

    dev = np.zeros((NT * NG, 2, 128))
    for t in range(NT):
        for g in range(NG):
            dev[t * NG + g, 0], dev[t * NG + g, 1] = forward(two_pi * ((kappa * t % 64) / 64 + (j * g % 4) / 4))
    high = ctab.astype(np.float32).astype(BF16).astype(np.float64)
    ctab3 = np.concatenate([high[:32], high[:32], (ctab - high)[:32], np.zeros((32, 128))])
    sums = np.concatenate([np.concatenate([stab] * 2, axis=0), np.concatenate([ctab3, np.zeros((128, 128))])], axis=1)
    return dict(
        table=table.astype(BF16),
        basis=basis.astype(BF16),
        pool=pool.astype(np.float32).astype(BF16),
        place=place.astype(BF16),
        rot=rot.astype(np.float32),
        sums=sums.astype(np.float32).astype(BF16),
        late=spread.astype(np.float32),
        dev=dev.astype(np.float32),
    )


ROW3, OWN, REC, SYN = 16, 22, 24, 26


def gelu_of_double(h):
    return h + h * jnp.tanh(h * (2.0 * GELU0 + 8.0 * GELU1 * (h * h)))


def dot(a, b):
    return jnp.dot(a, b, preferred_element_type=F32)


def exact(a, b):
    return jnp.dot(a, b, precision=PRECISE, preferred_element_type=F32)


XCHUNKS = 2


def kernel(
    x_hbm, mask_hbm, w_hbm, wp_hbm, bp_hbm, win_hbm, wout_hbm, wc_hbm, cp_hbm, cb_hbm,
    table_hbm, basis_hbm, pool_hbm, place_hbm, rot_hbm, sums_hbm, late_hbm, dev_hbm,
    out_ref,
    x_ref, mask_ref, wv, wp_ref, bp_ref, wint_ref, wout_ref, cp_ref, cb_ref,
    table, basis, pool, place, rot, sums, late, devv,
    xs, mf, fa, fb, wb, lhs, wpad, win, bias, pre_s, hid_s, parts_s, esend, erecv, csend, crecv, local, cx,
    lsem, ssem, rsem,
):
    t = lax.axis_index("tile")
    g = lax.axis_index("grp")

    count = [0]

    def load(src, dst):
        copy = pltpu.make_async_copy(src, dst, lsem.at[count[0]])
        count[0] += 1
        copy.start()
        return copy

    step_c = C // XCHUNKS
    get_mask = load(mask_hbm, mask_ref)
    get_x = [load(x_hbm.at[pl.ds(n * step_c, step_c)], x_ref.at[pl.ds(n * step_c, step_c)]) for n in range(XCHUNKS)]
    def at(tile, grp):
        return {"tile": tile, "grp": grp}

    row_there = {-1: t > 0, 1: t < NT - 1}
    column_there = {-1: g > 0, 1: g < NG - 1}

    def there(dt, dg):
        if dt and dg:
            return row_there[dt] & column_there[dg]
        return row_there[dt] if dt else column_there[dg]

    around = []
    for dt, dg in ((-1, -1), (-1, 1), (1, -1), (1, 1), (-1, 0), (1, 0), (0, -1), (0, 1)):
        around.append((dt, dg, at(lax.rem(t + (dt + NT), NT), lax.rem(g + (dg + NG), NG))))
    yc, xc, zlo = lax.rem(t, 8), lax.div(t, 16), lax.rem(lax.div(t, 8), 2)
    zc = 2 * g + zlo
    twin = [at(t + 1 - 2 * lax.rem(t, 2), g)]
    plane = []
    for dx in range(4):
        row = lax.rem(xc + dx, 4) * 16 + zlo * 8
        plane += [at(row + lax.rem(yc + 2 * dy, 8), g) for dy in range(4) if dx or dy]
    along_z = []
    for d in range(1, 8):
        z = lax.rem(zc + d, 8)
        along_z.append(at(xc * 16 + lax.rem(z, 2) * 8 + yc, lax.div(z, 2)))

    barrier = pltpu.get_barrier_semaphore()
    expected = jnp.int32(len(twin) + len(plane) + len(along_z))
    for dt, dg, device in around:
        expected = expected + there(dt, dg).astype(jnp.int32)

        @pl.when(there(dt, dg))
        def greet(device=device):
            pl.semaphore_signal(barrier, inc=1, device_id=device, device_id_type=MESH)

    for partner in along_z + plane + twin:
        pl.semaphore_signal(barrier, inc=1, device_id=partner, device_id_type=MESH)

    get_table = load(table_hbm, table)
    get_rot = load(rot_hbm, rot)
    get_w = [load(w_hbm.at[0], wv.at[0])]
    get_small = [
        load(wp_hbm, wp_ref), load(bp_hbm, bp_ref), load(win_hbm, wint_ref), load(wout_hbm, wout_ref),
        load(cp_hbm, cp_ref), load(cb_hbm, cb_ref), load(place_hbm, place), load(basis_hbm, basis),
    ]
    get_w.append(load(w_hbm.at[1], wv.at[1]))
    get_w.append(load(wc_hbm, wv.at[2]))
    get_late = [load(pool_hbm, pool), load(sums_hbm, sums), load(late_hbm, late), load(dev_hbm.at[t * NG + g], devv)]

    lane = lax.broadcasted_iota(jnp.int32, (64, 128), 1)
    mode = lane % 32
    in_a = (lane // 32) % 2 == 0
    in_a32 = in_a[:32]
    re_sign = jnp.where(lane < 64, -1.0, 1.0).astype(F32)

    def turned(v, row):
        return v * rot[row : row + 1, :] + pltpu.roll(v, 64, 1) * rot[row + 1 : row + 2, :]

    get_mask.wait()
    mf[...] = mask_ref[...].astype(F32)

    def mask_step(c, carry):
        xs[pl.ds(pl.multiple_of(c * PAD, 8), 64), :] = jnp.where(mask_ref[...] > 0, x_ref[c].astype(F32), 0.0)
        return carry

    for n in range(XCHUNKS):
        get_x[n].wait()
        lax.fori_loop(n * step_c, (n + 1) * step_c, mask_step, 0, unroll=4)

    def group_step(a, carry):
        for b in range(8):
            fa[a + 1, b] = xs[pl.ds(8 * a + b, 64, stride=PAD), :].astype(BF16)
        return carry

    lax.fori_loop(0, GROUPS, group_step, 0)

    get_table.wait()
    get_rot.wait()
    parts = dot(jnp.concatenate([fa[1:, b].reshape(512, 128) for b in range(8)], axis=1), table[...])
    total = turned(parts[:64], 0)
    for a in range(1, GROUPS):
        total = total + turned(parts[a * 64 : (a + 1) * 64], 2 * a)

    def remote(src, dst, number, device):
        return pltpu.make_async_remote_copy(
            src_ref=src, dst_ref=dst, send_sem=ssem.at[number], recv_sem=rsem.at[number],
            device_id=device, device_id_type=MESH,
        )

    def prepare(l):
        get_w[l].wait()

        def prepare_step(n, carry):
            rows = pl.ds(pl.multiple_of(n * 256, 256), 256)
            late_rows = pl.ds(pl.multiple_of(1024 + n * 256, 256), 256)
            wb[l, rows, :128] = jnp.concatenate([wv[l, 0, rows, :], wv[l, 1, rows, :]], axis=1).astype(BF16)
            wb[l, rows, 128:] = jnp.concatenate([wv[l, 0, late_rows, :], wv[l, 1, late_rows, :]], axis=1).astype(BF16)
            return carry

        lax.fori_loop(0, 4, prepare_step, 0)

    def exchange(l, total, beside):
        whole = turned(total, OWN)
        whole = whole + pltpu.roll(whole, 96, 1)
        packed = jnp.where(in_a32, whole[:32], pltpu.roll(whole[32:], 32, 1))
        esend[l, 1] = packed.astype(BF16)
        esend[l, 0] = jnp.where(in_a32, total[:32], pltpu.roll(total[32:], 32, 1)).astype(BF16)
        esend[l, 2] = jnp.where(in_a32, pltpu.roll(total[:32], 96, 1), total[32:]).astype(BF16)
        sends = []
        for n, (dt, dg, device) in enumerate(around):
            sends.append(remote(esend.at[l, dg + 1], erecv.at[l, 1 - dt, 1 - dg], 8 * l + n, device))
        for (dt, dg, _), send in zip(around, sends):
            pl.when(there(dt, dg))(send.start)
        beside()
        for (dt, dg, _), send in zip(around, sends):
            pl.when(there(dt, dg))(send.wait_send)
            pl.when(there(-dt, -dg))(send.wait_recv)
        rows = (t > 0, None, t < NT - 1)
        total = None
        for r in range(3):
            from_left = jnp.where(g > 0, erecv[l, r, 0].astype(F32), 0.0)
            from_right = jnp.where(g < NG - 1, erecv[l, r, 2].astype(F32), 0.0)
            middle = packed if r == 1 else erecv[l, r, 1].astype(F32)
            one = turned(middle + from_left + turned(from_right, REC), ROW3 + 2 * r)
            if rows[r] is not None:
                one = jnp.where(rows[r], one, 0.0)
            total = one if total is None else total + one
        return jnp.concatenate([total, pltpu.roll(total, 96, 1)], axis=0)

    def mix(l, u):
        sides = jnp.concatenate([u, pltpu.roll(u, 64, 1) * re_sign], axis=0)
        wide_a = jnp.concatenate([in_a, in_a], axis=0)
        both = jnp.concatenate(
            [jnp.where(wide_a, sides, 0.0), jnp.where(wide_a, 0.0, pltpu.roll(sides, 32, 1))], axis=0
        ).astype(BF16)
        acc = jnp.zeros((64, 128), F32)
        for block in range(4):
            o = dot(wb[l, block * 256 : (block + 1) * 256, :], both)
            for n in range(4):
                acc = jnp.where(mode % 16 == block * 4 + n, o[n * 64 : (n + 1) * 64], acc)
        return jnp.where(mode < 16, acc, pltpu.roll(acc, 96, 1))

    def layer(l, src, dst, v, matrix, finish):
        swapped = pltpu.roll(v, 64, 1)

        def synthesis(a):
            row = SYN + 2 * a
            return v * rot[row : row + 1, :] + swapped * rot[row + 1 : row + 2, :]

        fixed = wpad[l]
        whole = synthesis(0) + fixed
        rest = whole - whole.astype(BF16).astype(F32)
        fixed = fixed + jnp.where(lane == 64, pltpu.roll(rest, 64, 1), 0.0)
        for a in range(GROUPS):
            lhs[a] = (synthesis(a) + fixed).astype(BF16)

        def first(a, n):
            rhs = [
                jnp.concatenate([basis[b, :32], src[a + 1, b, :32], basis[b, 32:], src[a + 1, b, 32:]], axis=0)
                for b in (2 * n, 2 * n + 1)
            ]
            return dot(lhs[a], jnp.concatenate(rhs, axis=1))

        def second(pre):
            return dot(win[l], gelu_of_double(pre).astype(BF16))

        def third(hid, row):
            sea = [jnp.broadcast_to(mf[pl.ds(row + b, 1), :], (16, 128)).astype(BF16) for b in range(2)]
            sea = jnp.concatenate([jnp.concatenate(sea, axis=1)] * 4, axis=0)
            return dot(wout_ref[l], gelu_of_double(hid).astype(BF16)).astype(BF16) * sea

        for a in range(GROUPS + 1):
            for n in range(4):
                at_step, m = 4 * a + n, (n + 2) % 4
                if a < GROUPS:
                    pre_s[n] = first(a, n)
                if a > 0:
                    new = third(hid_s[n], 8 * (a - 1) + 2 * n)
                if 2 <= at_step < 4 * GROUPS + 2:
                    hid_s[m] = second(pre_s[m])
                if a > 0:
                    dst[a, 2 * n] = new[:, :128]
                    dst[a, 2 * n + 1] = new[:, 128:]
                if a > 1 and n < 2:
                    half = slice(512 * n, 512 * n + 512)
                    piece = dot(jnp.concatenate([dst[a - 1, b] for b in range(4 * n, 4 * n + 4)], axis=1), matrix[half, :])
                    parts_s[a - 1] = piece if n == 0 else parts_s[a - 1] + piece
        parts_s[GROUPS] = dot(jnp.concatenate([dst[GROUPS, b] for b in range(8)], axis=1), matrix[...])

        return finish([parts_s[a + 1] for a in range(GROUPS)])

    def analysis(parts):
        total = turned(parts[0], 0)
        for a in range(1, GROUPS):
            total = total + turned(parts[a], 2 * a)
        return total

    for copy in get_small:
        copy.wait()
    eye = lax.broadcasted_iota(jnp.int32, (64, 64), 0) == lax.broadcasted_iota(jnp.int32, (64, 64), 1)

    def column(row):
        return jnp.broadcast_to(jnp.sum(jnp.where(eye, row, 0.0), axis=1, keepdims=True), (64, 128))

    for l in range(2):
        wpad[l] = 0.5 * dot(wp_ref[l], place[...]) + jnp.where(lane == 0, 0.5 * column(bp_ref[l : l + 1, :]), 0.0)
        win[l] = (0.5 * wint_ref[l].astype(F32)).T.astype(BF16)
    bias[...] = column(cb_ref[...])

    pl.semaphore_wait(barrier, expected)
    u = exchange(0, total, lambda: prepare(0))
    v = mix(0, u)
    total = layer(0, fa, fb, v, table, analysis)
    u = exchange(1, total, lambda: prepare(1))
    v = mix(1, u)
    for copy in get_late:
        copy.wait()

    def pooled(parts):
        total = jnp.zeros((64, 128), F32)
        for a in range(GROUPS):
            total = total + jnp.where(lane // 8 == a // 2, parts[a], 0.0)
        return total

    coarse = layer(1, fb, fa, v, pool, pooled) * (1.0 / 256.0)

    cos, sin = devv[0:1, :], devv[1:2, :]
    high = coarse.astype(BF16).astype(F32)
    split = jnp.where(lane < 32, high, pltpu.roll(coarse - high, 32, 1) + pltpu.roll(high, 64, 1))
    part = dot(split.astype(BF16), sums[:128, 512:])
    part = part * cos + pltpu.roll(part, 64, 1) * sin
    acc = jnp.where(in_a32, part[:32], part[32:])
    slot = 0
    for stage, peers in enumerate((twin, plane, along_z)):
        csend[stage] = acc.astype(BF16)
        sends = []
        for peer in peers:
            sends.append(remote(csend.at[stage], crecv.at[slot], 16 + stage, peer))
            slot += 1
        for s in sends:
            s.start()
        if stage == 1:
            local[...] = exact(cp_ref[...], exact(coarse, late[...])) + jnp.concatenate([bias[...]] * 4, axis=1)
            prepare(2)
        if stage == 2:
            def back_step(a, carry):
                for b in range(8):
                    xs[pl.ds(8 * a + b, 64, stride=PAD), :] = fa[a + 1, b].astype(F32)
                return carry

            lax.fori_loop(0, GROUPS, back_step, 0)
        landed = crecv.at[pl.ds(slot - len(peers), len(peers))]
        for sem in (ssem, rsem):
            pltpu.make_async_copy(landed, landed, sem.at[16 + stage]).wait()
        for n in range(slot - len(peers), slot):
            acc = acc + crecv[n].astype(F32)
    u = jnp.concatenate([acc, pltpu.roll(acc, 96, 1)], axis=0)
    v = mix(2, u)
    v = v * cos - pltpu.roll(v, 64, 1) * sin
    high = v.astype(BF16)
    split = jnp.concatenate([high, (v - high.astype(F32)).astype(BF16)], axis=1)
    full = dot(split, sums[:, :512]) + local[...]
    for n in range(4):
        cx[n] = full[:, n * 128 : (n + 1) * 128]

    def final_step(c, carry):
        rows = []
        for n in range(4):
            fix = jnp.broadcast_to(cx[n, pl.ds(c, 1), :], (16, 128))
            base = pl.multiple_of(c * PAD, 8)
            rows.append(xs[pl.ds(base + 16 * n, 16), :] + fix * mf[16 * n : 16 * (n + 1), :])
        out_ref[c] = jnp.concatenate(rows, axis=0).astype(BF16)
        return carry

    lax.fori_loop(0, C, final_step, 0, unroll=4)


def local_program(consts, x, mask, w, wp, bp, win, wout, wc, cp, cb):
    hbm = pl.BlockSpec(memory_space=pltpu.HBM)
    n_remote = 16 + 3
    names = ["table", "basis", "pool", "place", "rot", "sums", "late", "dev"]
    return pl.pallas_call(
        kernel,
        out_shape=jax.ShapeDtypeStruct((C, TX, TY), BF16),
        in_specs=[hbm] * (10 + len(names)),
        out_specs=pl.BlockSpec(memory_space=pltpu.VMEM),
        scratch_shapes=[
            pltpu.VMEM((C, TX, TY), BF16),
            pltpu.VMEM((TX, TY), jnp.int32),
            pltpu.VMEM((3, 2, 2048, 64), F32),
            pltpu.VMEM((2, C, C), BF16),
            pltpu.VMEM((2, C), F32),
            pltpu.VMEM((2, C, F), BF16),
            pltpu.VMEM((2, C, F), BF16),
            pltpu.VMEM((C, C), F32),
            pltpu.VMEM((1, C), F32),
            pltpu.VMEM((1024, 128), BF16),
            pltpu.VMEM((8, 64, 128), BF16),
            pltpu.VMEM((1024, 128), BF16),
            pltpu.VMEM((64, 128), BF16),
            pltpu.VMEM((48, 128), F32),
            pltpu.VMEM((256, 640), BF16),
            pltpu.VMEM((128, 512), F32),
            pltpu.VMEM((2, 128), F32),
            pltpu.VMEM((C * PAD, 128), F32),
            pltpu.VMEM((TX, TY), F32),
            pltpu.VMEM((GROUPS + 1, 8, C, 128), BF16),
            pltpu.VMEM((GROUPS + 1, 8, C, 128), BF16),
            pltpu.VMEM((3, 1024, 256), BF16),
            pltpu.VMEM((GROUPS, C, 128), BF16),
            pltpu.VMEM((2, C, 128), F32),
            pltpu.VMEM((2, F, C), BF16),
            pltpu.VMEM((C, 128), F32),
            pltpu.VMEM((4, C, 256), F32),
            pltpu.VMEM((4, F, 256), F32),
            pltpu.VMEM((GROUPS + 1, C, 128), F32),
            pltpu.VMEM((2, 3, 32, 128), BF16),
            pltpu.VMEM((2, 3, 3, 32, 128), BF16),
            pltpu.VMEM((3, 32, 128), BF16),
            pltpu.VMEM((23, 32, 128), BF16),
            pltpu.VMEM((C, 512), F32),
            pltpu.VMEM((4, C, 128), F32),
            pltpu.SemaphoreType.DMA((21,)),
            pltpu.SemaphoreType.DMA((n_remote,)),
            pltpu.SemaphoreType.DMA((n_remote,)),
        ],
        compiler_params=pltpu.CompilerParams(
            collective_id=0, has_side_effects=True, vmem_limit_bytes=48000 * 1024
        ),
        name="ocean",
    )(
        *[
            pltpu.with_memory_space_constraint(v, pltpu.HBM)
            for v in (
                x, mask, w.reshape(2, 2, 2048, 64), wp, bp, jnp.swapaxes(win, 1, 2), wout,
                wc.reshape(2, 2048, 64), cp, cb.reshape(1, 64), *[consts[name] for name in names],
            )
        ]
    )


def solution(mesh):
    consts = constants()

    def body(*args):
        return local_program({k: jnp.asarray(v) for k, v in consts.items()}, *args)

    placed = (P(None, "tile", "grp"), P("tile", "grp"), P(), P(), P(), P(), P(), P(), P(), P())
    return jax.shard_map(body, mesh=mesh, in_specs=placed, out_specs=P(None, "tile", "grp"), check_vma=False)
```
